32 devices in a mesh: feat: 8 (over z, y), pair: 4 (over x, core).
Axes of the slice: x: 2, y: 2, z: 4, core: 2. Of those that a mesh axis runs over, the one named last changes fastest.
Arguments:
- in_factors: bfloat16 [512, 2, 512, 256], P(('feat', 'pair')), may hold values from -6 to 6
- out_factors: bfloat16 [512, 2, 512, 256], P(('feat', 'pair')), may hold values from -0.26367188 to 0.26367188
- token_counts: int32 [512, 2], P(('feat', 'pair')), may hold values from 1 to 512, as said below
- slot_pair: int32 [4, 128], P('pair'), may hold values from 0 to 127, each once within a row
- factor_panels: float32 [65536, 1536], P('feat'), as said below
Outputs:
- reduced: float32 [512, 65536], P('pair', 'feat')
The draws below stay inside these ranges and needn't reach their ends.
Inputs may be any that keep to these rules, and one draw needn't show every extreme that they name: `token_counts`: column 0 counts the chosen response's tokens, column 1 the rejected one's; positions at or beyond the count are padding. `slot_pair`: each row is a permutation of 0 to 127. `factor_panels`: entries above the diagonal in the unknowns' order are zero: rows of panel j hold zeros in the columns of panels after j, and D_k has a positive diagonal.
All inputs are finite; a program needn't handle non-finite values.
Results may differ from the reference program's by a relative error of at most 0.0003.
Values sent between devices are 32-bit elements; how exact they have to be, the bound alone decides.
A program may use at most 128 MiB of HBM per device.

```python
import jax
import jax.numpy as jnp
from jax import lax

R = 256
F = 65536
LMAX = 512
PAIR_SUB = 4
PANEL = 512
PANELS = 3
BLOCKS = 8
GROUPS = 4
SLOTS = 16
PG = 128
PAIRS = 512
ROWS_DEV = 8192


def draw_token_counts(key, part):
    key_counts, key_full, key_side, key_short = jax.random.split(jax.random.fold_in(key, 11), 4)
    counts = jax.random.randint(key_counts, (PAIRS, 2), 1, LMAX + 1)
    full_row = jax.random.randint(key_full, (), 0, PAIRS)
    full_side = jax.random.randint(key_side, (), 0, 2)
    short_row = (full_row + 1 + jax.random.randint(key_short, (), 0, PAIRS - 1)) % PAIRS
    row_index = lax.broadcasted_iota(jnp.int32, (PAIRS, 2), 0)
    side_index = lax.broadcasted_iota(jnp.int32, (PAIRS, 2), 1)
    counts = jnp.where((row_index == short_row) & (side_index == full_side), 1, counts)
    counts = jnp.where((row_index == full_row) & (side_index == full_side), LMAX, counts)
    return counts.astype(jnp.int32)


def draw_factor_panels(key, part):
    key_noise, key_diag = jax.random.split(jax.random.fold_in(key, 23), 2)
    shape = (F, PANELS * PANEL)
    row_index = lax.broadcasted_iota(jnp.int32, shape, 0)
    col_index = lax.broadcasted_iota(jnp.int32, shape, 1)
    block_index = row_index // (F // BLOCKS)
    offset = row_index % (F // BLOCKS)
    row_panel = jnp.where((block_index < PANELS) & (offset < PANEL), block_index, PANELS)
    col_panel = col_index // PANEL
    col_offset = col_index % PANEL
    noise = jax.random.normal(key_noise, shape, jnp.float32)
    diag_values = jax.random.uniform(key_diag, shape, jnp.float32, 1.0, 2.0)
    inside = row_panel == col_panel
    lower = inside & (offset > col_offset)
    on_diag = inside & (offset == col_offset)
    below = row_panel > col_panel
    values = jnp.where(below, noise / jnp.sqrt(jnp.float32(PANELS * PANEL)), 0.0)
    values = jnp.where(lower, noise * 0.6 / jnp.sqrt(jnp.float32(PANEL)), values)
    values = jnp.where(on_diag, diag_values, values)
    return values.astype(jnp.float32)


def block_scale(rng, shape, cuts, low, high):
    loudness = 1.0
    for dim, shards_of in cuts:
        draws = jax.random.uniform(jax.random.fold_in(jax.random.fold_in(rng, 6), dim), (shards_of,), jnp.float32, low / len(cuts), high / len(cuts))
        loudness = loudness * jnp.repeat(jnp.exp(draws), shape[dim] // shards_of).reshape((-1,) + (1,) * (len(shape) - 1 - dim))
    return loudness


def normal_values(stream_key, dims, width, most, cuts=(), held_as=jnp.bfloat16):
    drawn = jax.random.normal(stream_key, dims, jnp.float32) * width
    if len(cuts) > 0:
        drawn = block_scale(stream_key, dims, cuts, -0.22, 0.18) * drawn
    return jnp.clip(drawn, min=-most, max=most).astype(held_as)


def setup_inputs(seed: int = 0) -> dict:
    key_of = jax.random.split(jax.random.key(seed), 6)
    in_factors = normal_values(key_of[0], (PAIRS, 2, LMAX, R), 1.0, 6.0, ((0, 32),))
    out_factors = normal_values(key_of[1], (PAIRS, 2, LMAX, R), (LMAX ** -0.5), 0.26367188, ((0, 32),))
    token_counts = draw_token_counts(jax.random.fold_in(key_of[5], 71), 0)
    slot_pair = jax.vmap(lambda own: jax.random.permutation(own, PG))(jax.random.split(key_of[3], GROUPS)).reshape((GROUPS, PG)).astype(jnp.int32)
    factor_panels = draw_factor_panels(jax.random.fold_in(key_of[5], 71), 0)
    return {"in_factors": in_factors, "out_factors": out_factors, "token_counts": token_counts, "slot_pair": slot_pair, "factor_panels": factor_panels}


def block_gradients(pieces):
    signed_block, input_block = pieces
    result = jnp.einsum('ksti,kstj->kij', signed_block.astype(jnp.float32), input_block.astype(jnp.float32), precision=lax.Precision.HIGHEST)
    return result.reshape(signed_block.shape[0], R * R)

def reference(in_factors, out_factors, token_counts, slot_pair, factor_panels):
    positions = lax.broadcasted_iota(jnp.int32, (PAIRS, 2, LMAX), 2)
    side_index = lax.broadcasted_iota(jnp.int32, (PAIRS, 2, LMAX), 1)
    weights = jnp.where(positions < token_counts[:, :, None], jnp.where(side_index == 0, 1.0, -1.0), 0.0).astype(jnp.bfloat16)
    signed = out_factors * weights[..., None]
    blocked = (signed.reshape(PAIRS // SLOTS, SLOTS, 2, LMAX, R), in_factors.reshape(PAIRS // SLOTS, SLOTS, 2, LMAX, R))
    gradients = lax.map(block_gradients, blocked).reshape(PAIRS, R * R)
    ordered = gradients.reshape(BLOCKS, GROUPS, GROUPS, PAIR_SUB, R * R).transpose(2, 0, 1, 3, 4).reshape(GROUPS, PG, R * R)
    group_index = lax.broadcasted_iota(jnp.int32, (GROUPS, PG), 0)
    right_side = jnp.zeros((GROUPS, PG, R * R), jnp.float32).at[group_index, slot_pair].set(ordered).reshape(PAIRS, R * R)
    for k in range(PANELS):
        start = k * ROWS_DEV
        panel_cols = factor_panels[:, k * PANEL:(k + 1) * PANEL]
        diagonal = panel_cols[start:start + PANEL]
        solved = jax.scipy.linalg.solve_triangular(diagonal, right_side[:, start:start + PANEL].T, lower=True).T
        update = jnp.dot(solved.astype(jnp.float32), panel_cols.T.astype(jnp.float32), precision=lax.Precision.HIGHEST, preferred_element_type=jnp.float32)
        right_side = right_side - update
        right_side = right_side.at[:, start:start + PANEL].set(solved)
    return right_side
```

```python
import functools

import jax
import jax.numpy as jnp
from jax import lax
from jax.experimental import pallas as pl
from jax.experimental.pallas import tpu as pltpu
from jax.sharding import PartitionSpec as P

PANEL = 512
PANELS = 3
CHUNKS = 4
NT = (((1,), (1,)), ((), ()))


def dot_exact(a, b):
    return lax.dot_general(
        a, b, NT, precision=lax.Precision.HIGHEST, preferred_element_type=jnp.float32
    )


def chain_kernel(n_feat, head_ref, inverse_ref, lead_ref, out_ref, held, send_sem, recv_sem):
    feat = lax.axis_index("feat")
    pair = lax.axis_index("pair")
    level = feat // 2
    levels = n_feat // 2
    partner = feat + 1 - 2 * lax.rem(feat, 2)
    rows = head_ref.shape[0] // CHUNKS

    barrier = pltpu.get_barrier_semaphore()

    def greet(target):
        pl.semaphore_signal(
            barrier, inc=1, device_id=(target, pair), device_id_type=pl.DeviceIdType.MESH
        )

    greet(partner)

    @pl.when(level > 0)
    def _():
        greet(feat - 2)

    @pl.when(level + 1 < levels)
    def _():
        greet(feat + 2)

    below = jnp.where(level > 0, 1, 0)
    above = jnp.where(level + 1 < levels, 1, 0)
    pl.semaphore_wait(barrier, 1 + below + above)

    def piece(k, c, way, target):
        part = held.at[pl.ds(c * rows, rows), pl.ds(k * PANEL, PANEL)]
        return pltpu.make_async_remote_copy(
            src_ref=part,
            dst_ref=part,
            send_sem=send_sem.at[k, c, way],
            recv_sem=recv_sem.at[k, c],
            device_id=(target, pair),
            device_id_type=pl.DeviceIdType.MESH,
        )

    def routes(k):
        top = k // 2
        return (
            (0, feat == k, partner),
            (1, (level >= top) & (level + 1 < levels), feat + 2),
            (2, (level <= top) & (level > 0), feat - 2),
        )

    for k in range(PANELS):

        @pl.when(feat == k)
        def _():
            current = head_ref[...]
            if k > 0:
                current = current - dot_exact(held[:, : k * PANEL], lead_ref[:, : k * PANEL])
            held[:, k * PANEL : (k + 1) * PANEL] = dot_exact(current, inverse_ref[...])

        for c in range(CHUNKS):

            @pl.when(feat != k)
            def _():
                piece(k, c, 0, partner).wait_recv()

            for way, active, target in routes(k):

                @pl.when(active)
                def _():
                    piece(k, c, way, target).start()

    out_ref[...] = held[...]
    for k in range(PANELS):
        for c in range(CHUNKS):
            for way, active, target in routes(k):

                @pl.when(active)
                def _():
                    piece(k, c, way, target).wait_send()


def solve_chain(head, inverse, lead, n_feat):
    pairs = head.shape[0]
    return pl.pallas_call(
        functools.partial(chain_kernel, n_feat),
        out_shape=jax.ShapeDtypeStruct((pairs, PANELS * PANEL), jnp.float32),
        in_specs=[pl.BlockSpec(memory_space=pltpu.VMEM)] * 3,
        out_specs=pl.BlockSpec(memory_space=pltpu.VMEM),
        scratch_shapes=[
            pltpu.VMEM((pairs, PANELS * PANEL), jnp.float32),
            pltpu.SemaphoreType.DMA((PANELS, CHUNKS, 3)),
            pltpu.SemaphoreType.DMA((PANELS, CHUNKS)),
        ],
        compiler_params=pltpu.CompilerParams(
            collective_id=0, has_side_effects=True, vmem_limit_bytes=40 * 1024 * 1024
        ),
    )(head, inverse, lead)


def per_device(in_factors, out_factors, token_counts, slot_pair, factor_panels):
    slot_count, side_count, token_depth, proj_rank = in_factors.shape
    n_pair = lax.axis_size("pair")
    n_feat = lax.axis_size("feat")
    per_group = slot_count // n_pair
    row_count = factor_panels.shape[0]
    block = row_count // proj_rank
    feat_index = lax.axis_index("feat")
    positions = lax.broadcasted_iota(jnp.int32, (slot_count, side_count, token_depth), 2)
    side_index = lax.broadcasted_iota(jnp.int32, (slot_count, side_count, token_depth), 1)
    weights = jnp.where(
        positions < token_counts[:, :, None], jnp.where(side_index == 0, 1.0, -1.0), 0.0
    ).astype(jnp.bfloat16)
    signed = out_factors * weights[..., None]
    gradients = jnp.einsum("ksti,kstj->kij", signed, in_factors, preferred_element_type=jnp.float32)
    gradients = gradients.reshape(n_pair, per_group, n_feat, block, proj_rank)
    group_pairs = slot_pair[0]
    pair_total = n_pair * n_feat * per_group
    outgoing = gradients.transpose(2, 0, 1, 3, 4).reshape(
        n_feat * n_pair, per_group, block, proj_rank
    )
    received = lax.all_to_all(
        outgoing, ("feat", "pair"), split_axis=0, concat_axis=1, tiled=True
    ).reshape(pair_total, row_count)

    own = jnp.minimum(feat_index, PANELS - 1)
    lead = factor_panels[:PANEL]
    identity = jnp.eye(PANEL, dtype=jnp.float32)
    diagonal = lax.dynamic_slice(lead, (0, own * PANEL), (PANEL, PANEL))
    diagonal = jnp.where(feat_index < PANELS, diagonal, identity)
    inverse = jax.scipy.linalg.solve_triangular(diagonal, identity, lower=True)

    pair_rows = lax.broadcasted_iota(jnp.int32, (pair_total, pair_total), 0)
    placement = (pair_rows == group_pairs[None, :]).astype(jnp.float32)
    right_side = jnp.dot(
        placement, received, precision=lax.Precision.HIGH, preferred_element_type=jnp.float32
    )
    solved = solve_chain(right_side[:, :PANEL], inverse, lead, n_feat)
    result = right_side - lax.dot_general(
        solved,
        factor_panels,
        NT,
        precision=lax.Precision.HIGH,
        preferred_element_type=jnp.float32,
    )
    own_solved = lax.dynamic_slice(solved, (0, own * PANEL), (pair_total, PANEL))
    head = jnp.where(feat_index < PANELS, own_solved, result[:, :PANEL])
    return lax.dynamic_update_slice(result, head, (0, 0))


def solution(mesh):
    return jax.shard_map(
        per_device,
        mesh=mesh,
        in_specs=(
            P(("feat", "pair"), None, None, None),
            P(("feat", "pair"), None, None, None),
            P(("feat", "pair"), None),
            P("pair", None),
            P("feat", None),
        ),
        out_specs=P("pair", "feat"),
        check_vma=False,
    )
```

```python
import functools

import jax
import jax.numpy as jnp
from jax import lax
from jax.experimental import pallas as pl
from jax.experimental.pallas import tpu as pltpu
from jax.sharding import PartitionSpec as P

PANEL = 512
PANELS = 3
CHUNKS = 4
SUB = 128
TILE = 256
TILE_SLOTS = 4
FIRST = 6
PER_STEP = 1
NT = (((1,), (1,)), ((), ()))


def dot_exact(a, b):
    return lax.dot_general(
        a, b, NT, precision=lax.Precision.HIGHEST, preferred_element_type=jnp.float32
    )


def mega_kernel(
    n_feat, n_pair, pad, heads_ref, place_ref, lead_ref, factor_ref, outgoing_ref,
    received_ref, update_ref, solved_ref,
    arrived, inverse, current, held, split, tiles,
    head_send, head_recv, chain_send, chain_recv, swap_send, swap_recv, own_sem, tile_sem,
):
    feat = lax.axis_index("feat")
    pair = lax.axis_index("pair")
    devices = n_feat * n_pair
    me = feat * n_pair + pair
    level = feat // 2
    levels = n_feat // 2
    parity = lax.rem(feat, 2)
    partner = feat + 1 - 2 * parity
    pairs = held.shape[0]
    rows = pairs // CHUNKS
    depth = PANELS * PANEL

    def remote(src, dst, send_sem, recv_sem, target):
        return pltpu.make_async_remote_copy(
            src_ref=src,
            dst_ref=dst,
            send_sem=send_sem,
            recv_sem=recv_sem,
            device_id=target,
            device_id_type=pl.DeviceIdType.MESH,
        )

    def tile_copy(t, slot):
        return pltpu.make_async_copy(
            factor_ref.at[pl.ds(t * TILE, TILE), :], tiles.at[slot], tile_sem.at[slot]
        )

    tile_count = factor_ref.shape[0] // TILE
    depth_ahead = min(TILE_SLOTS, tile_count)
    for t in range(depth_ahead):
        tile_copy(t, t).start()

    barrier = pltpu.get_barrier_semaphore()

    def greet(j, carry):
        target = lax.rem(me + j, devices)
        pl.semaphore_signal(
            barrier,
            inc=1,
            device_id=(target // n_pair, lax.rem(target, n_pair)),
            device_id_type=pl.DeviceIdType.MESH,
        )
        return carry

    lax.fori_loop(1, devices, greet, 0)
    pl.semaphore_wait(barrier, devices - 1)

    mine = pl.ds(pl.multiple_of(me * pad, pad), pad)

    def head_copy(k, b):
        at = k * n_pair + b
        return remote(
            heads_ref.at[pl.ds(at * pad, pad), :],
            arrived.at[mine, :],
            head_send.at[at],
            head_recv.at[me],
            (k, b),
        )

    for k in range(PANELS):
        for b in range(n_pair):

            @pl.when(me != k * n_pair + b)
            def _():
                head_copy(k, b).start()

    own_copy = pltpu.make_async_copy(outgoing_ref.at[me], received_ref.at[me], own_sem)
    own_copy.start()

    def swap(i):
        step = i + 1 if i >= devices - n_pair else i
        ring = step // n_pair
        shift = n_feat // 2 + (ring + 1) // 2 * (2 * (ring % 2) - 1)
        to_feat = lax.rem(feat + shift, n_feat)
        to_pair = lax.rem(pair + step % n_pair, n_pair)
        target = to_feat * n_pair + to_pair
        return remote(
            outgoing_ref.at[target],
            received_ref.at[me],
            swap_send.at[i],
            swap_recv.at[me],
            (to_feat, to_pair),
        )

    swaps = devices - 1
    issued = 0

    def issue(count):
        nonlocal issued
        for i in range(issued, min(issued + count, swaps)):
            swap(i).start()
        issued = min(issued + count, swaps)

    issue(FIRST)
    subs = PANEL // SUB

    @pl.when(feat < PANELS)
    def _():
        column = pl.multiple_of(feat * PANEL, PANEL)
        lines = lax.broadcasted_iota(jnp.int32, (SUB, SUB), 0)
        lanes = lax.broadcasted_iota(jnp.int32, (SUB, SUB), 1)
        eye = jnp.where(lines == lanes, 1.0, 0.0).astype(jnp.float32)
        for s in range(subs):
            inverse[s] = eye

        def group(g, work):
            base = pl.multiple_of(g * 8, 8)
            for r in range(8):
                for s in range(subs):
                    col = work[s][:, r : r + 1]
                    block = inverse[s, pl.ds(base, 8), :]
                    pivot = jnp.sum(
                        jnp.where(lines[:, :1] == base + r, col, 0.0), axis=0, keepdims=True
                    )
                    row = block[r : r + 1, :] / pivot
                    below = jnp.where(lines[:, :1] > base + r, col, 0.0)
                    old = inverse[s]
                    inverse[s] = jnp.where(lines == base + r, row, old - below * row)
            return tuple(pltpu.roll(w, SUB - 8, 1) for w in work)

        start = tuple(
            lead_ref[s * SUB : (s + 1) * SUB, pl.ds(column + s * SUB, SUB)] for s in range(subs)
        )
        lax.fori_loop(0, SUB // 8, group, start)

        own_head = pl.multiple_of((feat * n_pair + pair) * pad, pad)
        arrived[mine, :] = heads_ref[pl.ds(own_head, pad), :]

        def take(j, carry):
            source = lax.rem(me + j, devices)
            part = arrived.at[pl.ds(pl.multiple_of(source * pad, pad), pad), :]
            remote(part, part, head_send.at[0], head_recv.at[source], (feat, pair)).wait_recv()
            return carry

        lax.fori_loop(1, devices, take, 0)
        current[...] = jnp.dot(
            place_ref[...],
            arrived[...],
            precision=lax.Precision.HIGHEST,
            preferred_element_type=jnp.float32,
        )

    def piece(k, c, way, target):
        part = held.at[pl.ds(c * rows, rows), pl.ds(k * PANEL, PANEL)]
        return remote(
            part, part, chain_send.at[k, c, way], chain_recv.at[k, c], (target, pair)
        )

    def routes(k, c):
        top = k // 2
        side = k % 2 if c < CHUNKS // 2 else 1 - k % 2
        on_side = parity == side
        return (
            (0, (feat == k) | (on_side & (level != top)), partner),
            (1, on_side & (level >= top) & (level + 1 < levels), feat + 2),
            (2, on_side & (level <= top) & (level > 0), feat - 2),
        )

    for k in range(PANELS):

        @pl.when(feat == k)
        def _():
            left = current[...]
            if k > 0:
                left = left - dot_exact(held[:, : k * PANEL], lead_ref[:, : k * PANEL])
            for s in range(subs):
                part = left[:, s * SUB : (s + 1) * SUB]
                if s > 0:
                    part = part - dot_exact(
                        held[:, k * PANEL : k * PANEL + s * SUB],
                        lead_ref[s * SUB : (s + 1) * SUB, k * PANEL : k * PANEL + s * SUB],
                    )
                held[:, k * PANEL + s * SUB : k * PANEL + (s + 1) * SUB] = dot_exact(
                    part, inverse[s]
                )

        for c in range(CHUNKS):

            @pl.when(feat != k)
            def _():
                piece(k, c, 0, partner).wait_recv()

            for way, active, target in routes(k, c):

                @pl.when(active)
                def _():
                    piece(k, c, way, target).start()

            issue(PER_STEP)

    issue(swaps)
    whole = held[...]
    high = whole.astype(jnp.bfloat16)
    split[:pairs, :] = high
    split[pairs:, :] = (whole - high.astype(jnp.float32)).astype(jnp.bfloat16)
    solved_ref[...] = whole

    def multiply(t, carry):
        slot = lax.rem(t, depth_ahead)
        tile_copy(t, slot).wait()
        tile = tiles[slot]
        top = tile.astype(jnp.bfloat16)
        low = (tile - top.astype(jnp.float32)).astype(jnp.bfloat16)
        both = lax.dot_general(split[...], top, NT, preferred_element_type=jnp.float32)
        rest = lax.dot_general(split[:pairs, :], low, NT, preferred_element_type=jnp.float32)
        columns = pl.ds(pl.multiple_of(t * TILE, TILE), TILE)
        update_ref[:, columns] = both[:pairs] + (both[pairs:] + rest)

        @pl.when(t + depth_ahead < tile_count)
        def _():
            tile_copy(t + depth_ahead, slot).start()

        return carry

    lax.fori_loop(0, tile_count, multiply, 0)

    for k in range(PANELS):
        for b in range(n_pair):

            @pl.when(me != k * n_pair + b)
            def _():
                head_copy(k, b).wait_send()

        for c in range(CHUNKS):
            for way, active, target in routes(k, c):

                @pl.when(active)
                def _():
                    piece(k, c, way, target).wait_send()

    own_copy.wait()
    for i in range(swaps):
        swap(i).wait_send()

    def collect(j, carry):
        source = lax.rem(me + j, devices)
        part = received_ref.at[source]
        remote(part, part, swap_send.at[0], swap_recv.at[source], (feat, pair)).wait_recv()
        return carry

    lax.fori_loop(1, devices, collect, 0)


def exchange_and_solve(heads, place, lead, factor_panels, outgoing, n_feat, n_pair, pad):
    pairs = place.shape[0]
    devices = n_feat * n_pair
    vmem = pl.BlockSpec(memory_space=pltpu.VMEM)
    anywhere = pl.BlockSpec(memory_space=pl.ANY)
    dma = pltpu.SemaphoreType.DMA
    return pl.pallas_call(
        functools.partial(mega_kernel, n_feat, n_pair, pad),
        out_shape=(
            jax.ShapeDtypeStruct(outgoing.shape, jnp.float32),
            jax.ShapeDtypeStruct((pairs, factor_panels.shape[0]), jnp.float32),
            jax.ShapeDtypeStruct((pairs, PANELS * PANEL), jnp.float32),
        ),
        in_specs=[vmem, vmem, vmem, anywhere, anywhere],
        out_specs=(anywhere, vmem, vmem),
        scratch_shapes=[
            pltpu.VMEM((devices * pad, PANEL), jnp.float32),
            pltpu.VMEM((PANEL // SUB, SUB, SUB), jnp.float32),
            pltpu.VMEM((pairs, PANEL), jnp.float32),
            pltpu.VMEM((pairs, PANELS * PANEL), jnp.float32),
            pltpu.VMEM((2 * pairs, PANELS * PANEL), jnp.bfloat16),
            pltpu.VMEM((TILE_SLOTS, TILE, PANELS * PANEL), jnp.float32),
            dma((PANELS * n_pair,)),
            dma((devices,)),
            dma((PANELS, CHUNKS, 3)),
            dma((PANELS, CHUNKS)),
            dma((devices,)),
            dma((devices,)),
            dma,
            dma((TILE_SLOTS,)),
        ],
        compiler_params=pltpu.CompilerParams(
            collective_id=0, has_side_effects=True, vmem_limit_bytes=56 * 1024 * 1024
        ),
    )(heads, place, lead, factor_panels, outgoing)


def per_device(in_factors, out_factors, token_counts, slot_pair, factor_panels):
    slot_count, side_count, token_depth, proj_rank = in_factors.shape
    n_pair = lax.axis_size("pair")
    n_feat = lax.axis_size("feat")
    per_group = slot_count // n_pair
    row_count = factor_panels.shape[0]
    block = row_count // proj_rank
    feat_index = lax.axis_index("feat")
    positions = lax.broadcasted_iota(jnp.int32, (slot_count, side_count, token_depth), 2)
    side_index = lax.broadcasted_iota(jnp.int32, (slot_count, side_count, token_depth), 1)
    weights = jnp.where(
        positions < token_counts[:, :, None], jnp.where(side_index == 0, 1.0, -1.0), 0.0
    ).astype(jnp.bfloat16)
    signed = out_factors * weights[..., None]
    gradients = jnp.einsum("ksti,kstj->kij", signed, in_factors, preferred_element_type=jnp.float32)
    gradients = gradients.reshape(n_pair, per_group, n_feat, block, proj_rank)
    group_pairs = slot_pair[0]
    pair_total = n_pair * n_feat * per_group
    outgoing = gradients.transpose(2, 0, 1, 3, 4).reshape(
        n_feat * n_pair, per_group, block, proj_rank
    )
    pad = -(-per_group // 8) * 8
    slim = PANEL // proj_rank
    heads = jnp.stack([gradients[:, :, k, :slim, :] for k in range(PANELS)])
    heads = heads.reshape(PANELS, n_pair, per_group, PANEL)
    heads = jnp.pad(heads, ((0, 0), (0, 0), (0, pad - per_group), (0, 0)))
    heads = heads.reshape(PANELS * n_pair * pad, PANEL)
    spots = jnp.pad(
        group_pairs.reshape(n_feat * n_pair, per_group),
        ((0, 0), (0, pad - per_group)),
        constant_values=-1,
    ).reshape(-1)
    wide_rows = lax.broadcasted_iota(jnp.int32, (pair_total, spots.shape[0]), 0)
    place = (wide_rows == spots[None, :]).astype(jnp.float32)
    received, update, solved = exchange_and_solve(
        heads, place, factor_panels[:PANEL], factor_panels, outgoing, n_feat, n_pair, pad
    )
    received = received.reshape(pair_total, row_count)
    pair_rows = lax.broadcasted_iota(jnp.int32, (pair_total, pair_total), 0)
    placement = (pair_rows == group_pairs[None, :]).astype(jnp.float32)
    result = (
        jnp.dot(
            placement, received, precision=lax.Precision.HIGH, preferred_element_type=jnp.float32
        )
        - update
    )
    own = jnp.minimum(feat_index, PANELS - 1)
    own_solved = lax.dynamic_slice(solved, (0, own * PANEL), (pair_total, PANEL))
    head = jnp.where(feat_index < PANELS, own_solved, result[:, :PANEL])
    return lax.dynamic_update_slice(result, head, (0, 0))


def solution(mesh):
    return jax.shard_map(
        per_device,
        mesh=mesh,
        in_specs=(
            P(("feat", "pair"), None, None, None),
            P(("feat", "pair"), None, None, None),
            P(("feat", "pair"), None),
            P("pair", None),
            P("feat", None),
        ),
        out_specs=P("pair", "feat"),
        check_vma=False,
    )
```

```python
import functools

import jax
import jax.numpy as jnp
from jax import lax
from jax.experimental import pallas as pl
from jax.experimental.pallas import tpu as pltpu
from jax.sharding import PartitionSpec as P

PANEL = 512
PANELS = 3
CHUNKS = 4
SUB = 128
TILE = 256
TILE_SLOTS = 4
FIRST = 6
PER_STEP = 1
NT = (((1,), (1,)), ((), ()))


def dot_exact(a, b):
    return lax.dot_general(
        a, b, NT, precision=lax.Precision.HIGHEST, preferred_element_type=jnp.float32
    )


def mega_kernel(
    n_feat, n_pair, pad, heads_ref, place_ref, factor_ref, outgoing_ref,
    received_ref, update_ref, solved_ref,
    arrived, inverse, current, held, split, tiles, lead_ref,
    head_send, head_recv, chain_send, chain_recv, swap_send, swap_recv, own_sem, tile_sem, lead_sem,
):
    feat = lax.axis_index("feat")
    pair = lax.axis_index("pair")
    devices = n_feat * n_pair
    me = feat * n_pair + pair
    level = feat // 2
    levels = n_feat // 2
    parity = lax.rem(feat, 2)
    partner = feat + 1 - 2 * parity
    pairs = held.shape[0]
    rows = pairs // CHUNKS
    depth = PANELS * PANEL

    def remote(src, dst, send_sem, recv_sem, target):
        return pltpu.make_async_remote_copy(
            src_ref=src,
            dst_ref=dst,
            send_sem=send_sem,
            recv_sem=recv_sem,
            device_id=target,
            device_id_type=pl.DeviceIdType.MESH,
        )

    def tile_copy(t, slot):
        return pltpu.make_async_copy(
            factor_ref.at[pl.ds(t * TILE, TILE), :], tiles.at[slot], tile_sem.at[slot]
        )

    lead_copy = pltpu.make_async_copy(factor_ref.at[pl.ds(0, PANEL), :], lead_ref, lead_sem)
    lead_copy.start()
    tile_count = factor_ref.shape[0] // TILE
    depth_ahead = min(TILE_SLOTS, tile_count)
    for t in range(depth_ahead):
        tile_copy(t, t).start()

    barrier = pltpu.get_barrier_semaphore()

    def greet(j, carry):
        target = lax.rem(me + j, devices)
        pl.semaphore_signal(
            barrier,
            inc=1,
            device_id=(target // n_pair, lax.rem(target, n_pair)),
            device_id_type=pl.DeviceIdType.MESH,
        )
        return carry

    lax.fori_loop(1, devices, greet, 0)
    pl.semaphore_wait(barrier, devices - 1)

    mine = pl.ds(pl.multiple_of(me * pad, pad), pad)

    def head_copy(k, b):
        at = k * n_pair + b
        return remote(
            heads_ref.at[pl.ds(at * pad, pad), :],
            arrived.at[mine, :],
            head_send.at[at],
            head_recv.at[me],
            (k, b),
        )

    for k in range(PANELS):
        for b in range(n_pair):

            @pl.when(me != k * n_pair + b)
            def _():
                head_copy(k, b).start()

    per_group, block = received_ref.shape[1:3]

    def parcel(to_feat, to_pair):
        return outgoing_ref.at[
            pl.ds(to_pair * per_group, per_group),
            pl.ds(pl.multiple_of(to_feat * block, block), block),
            :,
        ]

    own_copy = pltpu.make_async_copy(parcel(feat, pair), received_ref.at[me], own_sem)
    own_copy.start()

    def swap(i):
        step = i + 1 if i >= devices - n_pair else i
        ring = step // n_pair
        shift = n_feat // 2 + (ring + 1) // 2 * (2 * (ring % 2) - 1)
        to_feat = lax.rem(feat + shift, n_feat)
        to_pair = lax.rem(pair + step % n_pair, n_pair)
        return remote(
            parcel(to_feat, to_pair),
            received_ref.at[me],
            swap_send.at[i],
            swap_recv.at[me],
            (to_feat, to_pair),
        )

    swaps = devices - 1
    issued = 0

    def issue(count):
        nonlocal issued
        for i in range(issued, min(issued + count, swaps)):
            swap(i).start()
        issued = min(issued + count, swaps)

    issue(FIRST)
    lead_copy.wait()
    subs = PANEL // SUB

    @pl.when(feat < PANELS)
    def _():
        column = pl.multiple_of(feat * PANEL, PANEL)
        lines = lax.broadcasted_iota(jnp.int32, (SUB, SUB), 0)
        lanes = lax.broadcasted_iota(jnp.int32, (SUB, SUB), 1)
        eye = jnp.where(lines == lanes, 1.0, 0.0).astype(jnp.float32)
        for s in range(subs):
            inverse[s] = eye

        def group(g, work):
            base = pl.multiple_of(g * 8, 8)
            for r in range(8):
                for s in range(subs):
                    col = work[s][:, r : r + 1]
                    block = inverse[s, pl.ds(base, 8), :]
                    pivot = jnp.sum(
                        jnp.where(lines[:, :1] == base + r, col, 0.0), axis=0, keepdims=True
                    )
                    row = block[r : r + 1, :] / pivot
                    below = jnp.where(lines[:, :1] > base + r, col, 0.0)
                    old = inverse[s]
                    inverse[s] = jnp.where(lines == base + r, row, old - below * row)
            return tuple(pltpu.roll(w, SUB - 8, 1) for w in work)

        start = tuple(
            lead_ref[s * SUB : (s + 1) * SUB, pl.ds(column + s * SUB, SUB)] for s in range(subs)
        )
        lax.fori_loop(0, SUB // 8, group, start)

        own_head = pl.multiple_of((feat * n_pair + pair) * pad, pad)
        arrived[mine, :] = heads_ref[pl.ds(own_head, pad), :]

        def take(j, carry):
            source = lax.rem(me + j, devices)
            part = arrived.at[pl.ds(pl.multiple_of(source * pad, pad), pad), :]
            remote(part, part, head_send.at[0], head_recv.at[source], (feat, pair)).wait_recv()
            return carry

        lax.fori_loop(1, devices, take, 0)
        current[...] = jnp.dot(
            place_ref[...],
            arrived[...],
            precision=lax.Precision.HIGHEST,
            preferred_element_type=jnp.float32,
        )

    def piece(k, c, way, target):
        part = held.at[pl.ds(c * rows, rows), pl.ds(k * PANEL, PANEL)]
        return remote(
            part, part, chain_send.at[k, c, way], chain_recv.at[k, c], (target, pair)
        )

    def routes(k, c):
        top = k // 2
        side = k % 2 if c < CHUNKS // 2 else 1 - k % 2
        on_side = parity == side
        return (
            (0, (feat == k) | (on_side & (level != top)), partner),
            (1, on_side & (level >= top) & (level + 1 < levels), feat + 2),
            (2, on_side & (level <= top) & (level > 0), feat - 2),
        )

    for k in range(PANELS):

        @pl.when(feat == k)
        def _():
            left = current[...]
            if k > 0:
                left = left - dot_exact(held[:, : k * PANEL], lead_ref[:, : k * PANEL])
            for s in range(subs):
                part = left[:, s * SUB : (s + 1) * SUB]
                if s > 0:
                    part = part - dot_exact(
                        held[:, k * PANEL : k * PANEL + s * SUB],
                        lead_ref[s * SUB : (s + 1) * SUB, k * PANEL : k * PANEL + s * SUB],
                    )
                held[:, k * PANEL + s * SUB : k * PANEL + (s + 1) * SUB] = dot_exact(
                    part, inverse[s]
                )

        for c in range(CHUNKS):

            @pl.when(feat != k)
            def _():
                piece(k, c, 0, partner).wait_recv()

            for way, active, target in routes(k, c):

                @pl.when(active)
                def _():
                    piece(k, c, way, target).start()

            issue(PER_STEP)

    issue(swaps)
    whole = held[...]
    high = whole.astype(jnp.bfloat16)
    split[:pairs, :] = high
    split[pairs:, :] = (whole - high.astype(jnp.float32)).astype(jnp.bfloat16)
    solved_ref[...] = whole

    def multiply(t, carry):
        slot = lax.rem(t, depth_ahead)
        tile_copy(t, slot).wait()
        tile = tiles[slot]
        top = tile.astype(jnp.bfloat16)
        low = (tile - top.astype(jnp.float32)).astype(jnp.bfloat16)
        both = lax.dot_general(split[...], top, NT, preferred_element_type=jnp.float32)
        rest = lax.dot_general(split[:pairs, :], low, NT, preferred_element_type=jnp.float32)
        columns = pl.ds(pl.multiple_of(t * TILE, TILE), TILE)
        update_ref[:, columns] = both[:pairs] + (both[pairs:] + rest)

        @pl.when(t + depth_ahead < tile_count)
        def _():
            tile_copy(t + depth_ahead, slot).start()

        return carry

    lax.fori_loop(0, tile_count, multiply, 0)

    for k in range(PANELS):
        for b in range(n_pair):

            @pl.when(me != k * n_pair + b)
            def _():
                head_copy(k, b).wait_send()

        for c in range(CHUNKS):
            for way, active, target in routes(k, c):

                @pl.when(active)
                def _():
                    piece(k, c, way, target).wait_send()

    own_copy.wait()
    for i in range(swaps):
        swap(i).wait_send()

    def collect(j, carry):
        source = lax.rem(me + j, devices)
        part = received_ref.at[source]
        remote(part, part, swap_send.at[0], swap_recv.at[source], (feat, pair)).wait_recv()
        return carry

    lax.fori_loop(1, devices, collect, 0)


def exchange_and_solve(heads, place, factor_panels, outgoing, n_feat, n_pair, pad):
    pairs = place.shape[0]
    block = factor_panels.shape[0] // outgoing.shape[2]
    per_group = outgoing.shape[0] // n_pair
    devices = n_feat * n_pair
    vmem = pl.BlockSpec(memory_space=pltpu.VMEM)
    anywhere = pl.BlockSpec(memory_space=pl.ANY)
    dma = pltpu.SemaphoreType.DMA
    return pl.pallas_call(
        functools.partial(mega_kernel, n_feat, n_pair, pad),
        out_shape=(
            jax.ShapeDtypeStruct(
                (devices, per_group, block, outgoing.shape[2]), jnp.float32
            ),
            jax.ShapeDtypeStruct((pairs, factor_panels.shape[0]), jnp.float32),
            jax.ShapeDtypeStruct((pairs, PANELS * PANEL), jnp.float32),
        ),
        in_specs=[vmem, vmem, anywhere, anywhere],
        out_specs=(anywhere, vmem, vmem),
        scratch_shapes=[
            pltpu.VMEM((devices * pad, PANEL), jnp.float32),
            pltpu.VMEM((PANEL // SUB, SUB, SUB), jnp.float32),
            pltpu.VMEM((pairs, PANEL), jnp.float32),
            pltpu.VMEM((pairs, PANELS * PANEL), jnp.float32),
            pltpu.VMEM((2 * pairs, PANELS * PANEL), jnp.bfloat16),
            pltpu.VMEM((TILE_SLOTS, TILE, PANELS * PANEL), jnp.float32),
            pltpu.VMEM((PANEL, PANELS * PANEL), jnp.float32),
            dma((PANELS * n_pair,)),
            dma((devices,)),
            dma((PANELS, CHUNKS, 3)),
            dma((PANELS, CHUNKS)),
            dma((devices,)),
            dma((devices,)),
            dma,
            dma((TILE_SLOTS,)),
            dma,
        ],
        compiler_params=pltpu.CompilerParams(
            collective_id=0, has_side_effects=True, vmem_limit_bytes=56 * 1024 * 1024
        ),
    )(heads, place, factor_panels, outgoing)


def finish_kernel(slim, keep_ref, placement_ref, own_ref, received_ref, update_ref, out_ref):
    rank = received_ref.shape[2]
    step = pl.program_id(0)
    placement = placement_ref[...]
    for i in range(received_ref.shape[1]):
        slab = received_ref[:, i, :]
        high = slab.astype(jnp.bfloat16)
        low = (slab - high.astype(jnp.float32)).astype(jnp.bfloat16)
        placed = jnp.dot(placement, high, preferred_element_type=jnp.float32) + jnp.dot(
            placement, low, preferred_element_type=jnp.float32
        )
        columns = slice(i * rank, (i + 1) * rank)
        value = placed - update_ref[:, columns]
        if i < slim:
            owner = (keep_ref[0:1, 0:1] > 0.5) & (step == 0)
            value = jnp.where(owner, own_ref[:, columns], value)
        out_ref[:, columns] = value


def place_and_subtract(received, placement, update, own_solved, keep):
    pairs, block, rank = received.shape
    vmem = pl.BlockSpec(memory_space=pltpu.VMEM)
    lines = 8
    return pl.pallas_call(
        functools.partial(finish_kernel, PANEL // rank),
        grid=(block // lines,),
        out_shape=jax.ShapeDtypeStruct(update.shape, jnp.float32),
        in_specs=[
            vmem,
            vmem,
            vmem,
            pl.BlockSpec((pairs, lines, rank), lambda t: (0, t, 0)),
            pl.BlockSpec((pairs, lines * rank), lambda t: (0, t)),
        ],
        out_specs=pl.BlockSpec((pairs, lines * rank), lambda t: (0, t)),
        compiler_params=pltpu.CompilerParams(vmem_limit_bytes=56 * 1024 * 1024),
    )(keep, placement, own_solved, received, update)


def per_device(in_factors, out_factors, token_counts, slot_pair, factor_panels):
    slot_count, side_count, token_depth, proj_rank = in_factors.shape
    n_pair = lax.axis_size("pair")
    n_feat = lax.axis_size("feat")
    per_group = slot_count // n_pair
    row_count = factor_panels.shape[0]
    block = row_count // proj_rank
    feat_index = lax.axis_index("feat")
    positions = lax.broadcasted_iota(jnp.int32, (slot_count, side_count, token_depth), 2)
    side_index = lax.broadcasted_iota(jnp.int32, (slot_count, side_count, token_depth), 1)
    weights = jnp.where(
        positions < token_counts[:, :, None], jnp.where(side_index == 0, 1.0, -1.0), 0.0
    ).astype(jnp.bfloat16)
    signed = out_factors * weights[..., None]
    gradients = jnp.einsum("ksti,kstj->kij", signed, in_factors, preferred_element_type=jnp.float32)
    outgoing = gradients
    gradients = gradients.reshape(n_pair, per_group, n_feat, block, proj_rank)
    group_pairs = slot_pair[0]
    pair_total = n_pair * n_feat * per_group
    pad = -(-per_group // 8) * 8
    slim = PANEL // proj_rank
    heads = jnp.stack([gradients[:, :, k, :slim, :] for k in range(PANELS)])
    heads = heads.reshape(PANELS, n_pair, per_group, PANEL)
    heads = jnp.pad(heads, ((0, 0), (0, 0), (0, pad - per_group), (0, 0)))
    heads = heads.reshape(PANELS * n_pair * pad, PANEL)
    spots = jnp.pad(
        group_pairs.reshape(n_feat * n_pair, per_group),
        ((0, 0), (0, pad - per_group)),
        constant_values=-1,
    ).reshape(-1)
    wide_rows = lax.broadcasted_iota(jnp.int32, (pair_total, spots.shape[0]), 0)
    place = (wide_rows == spots[None, :]).astype(jnp.float32)
    received, update, solved = exchange_and_solve(
        heads, place, factor_panels, outgoing, n_feat, n_pair, pad
    )
    own = jnp.minimum(feat_index, PANELS - 1)
    own_solved = lax.dynamic_slice(solved, (0, own * PANEL), (pair_total, PANEL))
    keep = jnp.broadcast_to((feat_index < PANELS).astype(jnp.float32), (8, 128))
    pair_rows = lax.broadcasted_iota(jnp.int32, (pair_total, pair_total), 0)
    placement = (pair_rows == group_pairs[None, :]).astype(jnp.bfloat16)
    return place_and_subtract(
        received.reshape(pair_total, block, proj_rank), placement, update, own_solved, keep
    )


def solution(mesh):
    return jax.shard_map(
        per_device,
        mesh=mesh,
        in_specs=(
            P(("feat", "pair"), None, None, None),
            P(("feat", "pair"), None, None, None),
            P(("feat", "pair"), None),
            P("pair", None),
            P("feat", None),
        ),
        out_specs=P("pair", "feat"),
        check_vma=False,
    )
```
